32 devices in a mesh: groups: 2 (over x), seq: 8 (over z, y), chan: 2 (over core).
Axes of the slice: x: 2, y: 2, z: 4, core: 2. Of those that a mesh axis runs over, the one named last changes fastest.
Arguments:
- stream: bfloat16 [4096, 2048], P(('groups', 'seq'), 'chan'), parts along dimension 0, may hold values from -6 to 6
- nucleotide_token_ids: int32 [4096], P(('groups', 'seq')), parts along dimension 0, may hold values from 4 to 11, as said below
- genome_length: int32 [2], P('groups'), parts along dimension 0, may hold values from 1024 to 2048
- embedding: bfloat16 [16, 2048], replicated, may hold values from -6 to 6
- attention_in: bfloat16 [2048, 3, 1024], P(None, None, 'chan'), may hold values from -0.125 to 0.125
- scan_input: bfloat16 [2048, 1024], P(None, 'chan'), may hold values from -0.125 to 0.125
- state_maps: bfloat16 [2048, 256], P(None, 'chan'), may hold values from -0.125 to 0.125
- step_weight: bfloat16 [2048, 8], P(None, 'chan'), may hold values from -0.125 to 0.125
- step_bias: float32 [8], P('chan'), may hold values from -1 to 1
- head_decay_speed: float32 [8], P('chan'), as said below
- attention_gain: float32 [1024], P('chan'), may hold values from 0.25 to 1.75
- scan_gain: float32 [1024], P('chan'), may hold values from 0.25 to 1.75
- out_weight: bfloat16 [1024, 2048], P('chan'), may hold values from -0.1875 to 0.1875
Outputs:
- block_out: bfloat16 [4096, 2048], P(('groups', 'seq'), 'chan'), parts along dimension 0
The draws below stay inside these ranges and needn't reach their ends.
There are 2 independent parts, one for each index of `groups`. The reference program is written for one: setup_inputs(seed, part) draws one part's arguments, and reference() takes and returns one part's arrays. A program takes and returns all parts, laid end to end along the dimension named above; an argument that names none is the same for every part. Nothing has to cross between parts.
Inputs may be any that keep to these rules, and one draw needn't show every extreme that they name: `nucleotide_token_ids`: positions below genome_length hold bases 7 to 10, except exactly three positions that hold 11, one in each third of the valid range; positions at or above genome_length hold 4. `head_decay_speed`: every entry lies between 1 / 20480 and 8 / 256.
All inputs are finite; a program needn't handle non-finite values.
Results may differ from the reference program's by a relative error of at most 0.0058.
Values may be sent and summed in bfloat16 or wider, within the bound.
A program may use at most 128 MiB of HBM per device.

```python
import math
import jax
import jax.numpy as jnp
import numpy as np
from jax import lax

D = 2048
HEADS = 8
HEAD_DIM = 128
STATE = 64
GROUPS = 2
VOCAB = 16
TOK_DEV = 256
LENGTH = 2048
WIDTH_H = 1024
N_SEQ = 8


def common_length(key):
    return LENGTH - jax.random.randint(jax.random.fold_in(key, 11), (), 0, LENGTH // 2 + 1)


def draw_genome_length(key, part):
    return common_length(key).reshape(1).astype(jnp.int32)


def draw_nucleotide_token_ids(key, part):
    valid_limit = common_length(key)
    position = jnp.arange(LENGTH, dtype=jnp.int32)
    bases = jax.random.randint(jax.random.fold_in(key, 12), (LENGTH,), 7, 11)
    third_part = valid_limit // 3
    offsets = jax.random.randint(jax.random.fold_in(key, 13), (3,), 0, 1 << 20) % third_part
    marked = jnp.arange(3, dtype=jnp.int32) * third_part + offsets
    is_marked = jnp.any(position[:, None] == marked[None, :], axis=1)
    tokens = jnp.where(is_marked, 11, bases)
    return jnp.where(position < valid_limit, tokens, 4).astype(jnp.int32)


def draw_head_decay_speed(key, part):
    ranking = jax.random.permutation(jax.random.fold_in(key, 21), HEADS)
    fast_count = HEADS // 2
    fast_heads = ranking < fast_count
    fast_rate = jnp.exp(jax.random.uniform(jax.random.fold_in(key, 22), (HEADS,), jnp.float32, math.log(4.0 / TOK_DEV), math.log(8.0 / TOK_DEV)))
    slow_rate = jnp.exp(jax.random.uniform(jax.random.fold_in(key, 23), (HEADS,), jnp.float32, math.log(0.1 / LENGTH), math.log(1.0 / LENGTH)))
    return jnp.where(fast_heads, fast_rate, slow_rate).astype(jnp.float32)


def shard_levels(own_key, shape, split, low, high):
    gain, own = 1.0, jax.random.fold_in(own_key, 6)
    for dim, parts in split:
        heights = jnp.exp(jax.random.uniform(jax.random.fold_in(own, dim), (parts,), jnp.float32, low / len(split), high / len(split)))
        gain = gain * jnp.repeat(heights, shape[dim] // parts).reshape([-1 if axis == dim else 1 for axis in range(len(shape))])
    return gain


def noise(key, extent, scale, limit, split=(), held_as=jnp.bfloat16):
    gain = shard_levels(key, extent, split, -0.22, 0.18) if split else 1.0
    result = jax.random.normal(key, extent, jnp.float32) * scale * gain
    return jnp.minimum(jnp.maximum(result, -limit), limit).astype(held_as)


def setup_inputs(seed: int = 0, part: int = 0) -> dict:
    splits = jax.random.split(jax.random.key(seed), 14)
    part_splits = jax.random.split(jax.random.fold_in(splits[13], part), 14)
    stream = noise(part_splits[0], (LENGTH, D), 1.0, 6.0, ((0, 8), (1, 2)))
    nucleotide_token_ids = draw_nucleotide_token_ids(jax.random.fold_in(jax.random.fold_in(splits[13], part), 71), part)
    genome_length = draw_genome_length(jax.random.fold_in(jax.random.fold_in(splits[13], part), 71), part)
    embedding = noise(splits[3], (VOCAB, D), 1.0, 6.0)
    attention_in = noise(splits[4], (D, 3, WIDTH_H), D ** -0.5, 0.125, ((2, 2),))
    scan_input = noise(splits[5], (D, WIDTH_H), D ** -0.5, 0.125, ((1, 2),))
    state_maps = noise(splits[6], (D, GROUPS * 2 * STATE), D ** -0.5, 0.125, ((1, 2),))
    step_weight = noise(splits[7], (D, HEADS), D ** -0.5, 0.125, ((1, 2),))
    step_bias = jnp.clip(jax.random.uniform(splits[8], (HEADS,), jnp.float32, -1.0, 1.0) * shard_levels(splits[8], (HEADS,), ((0, 2),), -0.4, 0.0), -1.0, 1.0)
    head_decay_speed = draw_head_decay_speed(jax.random.fold_in(splits[13], 71), part)
    attention_gain = jnp.clip(1.0 + 0.15 * jax.random.normal(splits[10], (WIDTH_H,), jnp.float32), 0.25, 1.75)
    scan_gain = jnp.clip(1.0 + 0.15 * jax.random.normal(splits[11], (WIDTH_H,), jnp.float32), 0.25, 1.75)
    out_weight = noise(splits[12], (WIDTH_H, D), WIDTH_H ** -0.5, 0.1875, ((0, 2),))
    return dict(stream=stream, nucleotide_token_ids=nucleotide_token_ids, genome_length=genome_length, embedding=embedding, attention_in=attention_in, scan_input=scan_input, state_maps=state_maps, step_weight=step_weight, step_bias=step_bias, head_decay_speed=head_decay_speed, attention_gain=attention_gain, scan_gain=scan_gain, out_weight=out_weight)


epsilon_norm = 1e-06
spike_logarithm = math.log(0.7)
unclear_nucleotide = 11

def normalize(values):
    return values * lax.rsqrt(lax.optimization_barrier(jnp.mean(values * values, axis=-1, keepdims=True)) + epsilon_norm)

def blocked(array_in):
    return array_in.reshape((N_SEQ, TOK_DEV) + array_in.shape[1:])

def circulate(passage, block_end):

    def advance(carry_state, element):
        factor, finish = element
        return (factor[:, None, None] * carry_state + finish, carry_state)
    zero_state = jnp.zeros(block_end.shape[1:], block_end.dtype)
    lap_state, _ = lax.scan(advance, zero_state, (passage, block_end))
    beside_all = jnp.prod(passage, axis=0)
    starting = lap_state / (1.0 - beside_all)[:, None, None]
    _, entering = lax.scan(advance, starting, (passage, block_end))
    return entering

def reference(stream, nucleotide_token_ids, genome_length, embedding, attention_in, scan_input, state_maps, step_weight, step_bias, head_decay_speed, attention_gain, scan_gain, out_weight):
    score_scale = 2.0 / math.sqrt(HEAD_DIM)
    valid_limit = genome_length[0]
    position = jnp.arange(LENGTH, dtype=jnp.int32)
    key_valid = position < valid_limit
    onehot = (nucleotide_token_ids[:, None] == jnp.arange(VOCAB, dtype=jnp.int32)[None, :]).astype(jnp.bfloat16)
    hidden = (stream.astype(jnp.float32) + jnp.dot(onehot, embedding, preferred_element_type=jnp.float32)).astype(jnp.bfloat16)
    projected = jnp.dot(hidden, attention_in.reshape(D, 3 * WIDTH_H), preferred_element_type=jnp.float32).reshape(LENGTH, 3, HEADS, HEAD_DIM)
    queries = normalize(projected[:, 0]).astype(jnp.bfloat16)
    keyset = normalize(projected[:, 1]).astype(jnp.bfloat16)
    valueset = projected[:, 2].astype(jnp.bfloat16)

    def attend(operands):
        query_head, key_head, value_head = operands
        scores = jnp.dot(query_head, key_head.T, preferred_element_type=jnp.float32) * score_scale
        weights = jnp.where(key_valid[None, :], jnp.exp(scores), 0.0)
        totals = lax.optimization_barrier(jnp.sum(weights, axis=1))
        numerator = jnp.dot(weights.astype(jnp.bfloat16), value_head, preferred_element_type=jnp.float32)
        return numerator / totals[:, None]
    attended = lax.map(attend, (jnp.swapaxes(queries, 0, 1), jnp.swapaxes(keyset, 0, 1), jnp.swapaxes(valueset, 0, 1)))
    attended = normalize(jnp.swapaxes(attended, 0, 1))
    inputs = jax.nn.silu(jnp.dot(hidden, scan_input, preferred_element_type=jnp.float32)).astype(jnp.bfloat16).reshape(LENGTH, HEADS, HEAD_DIM)
    state_rows = jax.nn.silu(jnp.dot(hidden, state_maps, preferred_element_type=jnp.float32)).astype(jnp.bfloat16).reshape(LENGTH, GROUPS, 2, STATE)
    group_of = np.arange(HEADS) // (HEADS // GROUPS)
    input_map = state_rows[:, group_of, 0]
    output_map = state_rows[:, group_of, 1]
    step_list = jax.nn.softplus(jnp.dot(hidden, step_weight, preferred_element_type=jnp.float32) + step_bias[None, :])
    usable_rows = key_valid.astype(jnp.float32)[:, None]
    spike_events = jnp.where(nucleotide_token_ids == unclear_nucleotide, spike_logarithm, 0.0)[:, None]
    logarithm_decay = usable_rows * (-head_decay_speed[None, :] * step_list + spike_events)
    used_steps = usable_rows * step_list
    log_blocks = blocked(logarithm_decay)
    step_blocks = blocked(used_steps)
    input_blocks = blocked(inputs).astype(jnp.float32)
    write_blocks = blocked(input_map).astype(jnp.float32)
    read_blocks = blocked(output_map).astype(jnp.float32)
    forward = jnp.cumsum(log_blocks, axis=1)
    backward = jnp.flip(jnp.cumsum(jnp.flip(log_blocks, 1), axis=1), 1)
    pass_forward = jnp.exp(forward[:, -1])
    pass_backward = jnp.exp(backward[:, 0])
    scaled_forward = ((jnp.exp(forward[:, -1:] - forward) * step_blocks)[..., None] * input_blocks).astype(jnp.bfloat16)
    scaled_backward = ((jnp.exp(backward[:, :1] - backward) * step_blocks)[..., None] * input_blocks).astype(jnp.bfloat16)
    end_forward = jnp.einsum('bthe,bths->bhes', scaled_forward.astype(jnp.float32), write_blocks)
    end_backward = jnp.einsum('bthe,bths->bhes', scaled_backward.astype(jnp.float32), write_blocks)
    enter_forward = circulate(pass_forward, end_forward)
    enter_backward = jnp.flip(circulate(jnp.flip(pass_backward, 0), jnp.flip(end_backward, 0)), 0)
    pairing = jnp.einsum('bths,buhs->bhtu', read_blocks, write_blocks)
    block_rows = jnp.arange(TOK_DEV)
    causal_mask = block_rows[:, None] >= block_rows[None, :]

    def strand(cumulative, allowed, entering):
        across = jnp.moveaxis(cumulative, 2, 1)
        exponent = across[:, :, :, None] - across[:, :, None, :]
        mixing = (pairing * jnp.exp(jnp.where(allowed, exponent, -jnp.inf)) * jnp.moveaxis(step_blocks, 2, 1)[:, :, None, :]).astype(jnp.bfloat16)
        local_part = jnp.einsum('bhtu,buhe->bthe', mixing.astype(jnp.float32), input_blocks)
        carried = jnp.exp(cumulative)[..., None] * jnp.einsum('bths,bhes->bthe', read_blocks, entering, precision=lax.Precision.HIGHEST)
        return local_part + carried
    scanned = strand(forward, causal_mask, enter_forward) + strand(backward, causal_mask.T, enter_backward)
    scanned = normalize(scanned.reshape(LENGTH, HEADS, HEAD_DIM))
    combined = (attention_gain.reshape(HEADS, HEAD_DIM) * attended + scan_gain.reshape(HEADS, HEAD_DIM) * scanned).astype(jnp.bfloat16).reshape(LENGTH, WIDTH_H)
    return (stream.astype(jnp.float32) + jnp.dot(combined, out_weight, preferred_element_type=jnp.float32)).astype(jnp.bfloat16)
```

```python
import functools
import math

import jax
import jax.numpy as jnp
from jax import lax
from jax.experimental import pallas as pl
from jax.experimental.pallas import tpu as pltpu
from jax.sharding import PartitionSpec as P

HEAD_DIM = 128
STATE = 64
EPS = 1e-06
SPIKE = math.log(0.7)
UNCLEAR = 11
F32 = jnp.float32
BF16 = jnp.bfloat16
MESH = pl.DeviceIdType.MESH


def mm(a, b):
    return lax.dot_general(a, b, (((1,), (0,)), ((), ())), preferred_element_type=F32)


def mm_nt(a, b):
    return lax.dot_general(a, b, (((1,), (1,)), ((), ())), preferred_element_type=F32)


def normed(v):
    return v * lax.rsqrt(jnp.mean(v * v, axis=-1, keepdims=True) + EPS)


def silu(v):
    return v / (1.0 + jnp.exp(-v))


def exact_mm(a, b):
    first = a.astype(BF16)
    rest = a - first.astype(F32)
    second = rest.astype(BF16)
    third = (rest - second.astype(F32)).astype(BF16)
    return mm(first, b) + (mm(second, b) + mm(third, b))


def kernel(
    n,
    stream,
    ids,
    glen,
    emb,
    watt,
    wscan,
    wstate,
    wstep,
    bias,
    speed,
    again,
    sgain,
    wout,
    out,
    emb_v,
    watt_v,
    wscan_v,
    wstate_v,
    wstep_v,
    wout_v,
    other_stream,
    hid,
    kvsend,
    kvrecv,
    qsend,
    qrecv,
    acc,
    attsend,
    attrecv,
    endsend,
    endrecv,
    entsend,
    entrecv,
    x_v,
    loc_v,
    comb_v,
    psend,
    precv,
    wsem,
    xs_send,
    xs_recv,
    kv_ss,
    kv_rs,
    q_ss,
    q_rs,
    at_ss,
    at_rs,
    en_ss,
    en_rs,
    er_ss,
    er_rs,
    ps_ss,
    ps_rs,
):
    rows, half = stream.shape
    heads = kvsend.shape[0]
    me = lax.axis_index("seq")
    chan = lax.axis_index("chan")
    partner = 1 - chan
    member = lax.rem(me, heads)
    base = me - member
    span = heads * HEAD_DIM
    rpd = span // n

    own_at = pl.multiple_of(chan * half, half)
    other_at = pl.multiple_of(partner * half, half)
    places = (own_at, other_at)

    emb_v[...] = jnp.zeros_like(emb_v)
    loads = {}

    def load(name, index, src, dst):
        copy = pltpu.make_async_copy(src, dst, wsem.at[index])
        copy.start()
        loads[name] = copy

    vocab = emb.shape[0]
    for i, at in enumerate(places):
        load(("emb", i), i, emb.at[:, pl.ds(at, half)], emb_v.at[i, pl.ds(0, vocab)])
    for j, part in enumerate((1, 2, 0)):
        for i, at in enumerate(places):
            load(
                ("att", part, i),
                2 + 2 * j + i,
                watt.at[part, pl.ds(at, half)],
                watt_v.at[part, i],
            )
    for i, at in enumerate(places):
        load(("state", i), 8 + i, wstate.at[pl.ds(at, half)], wstate_v.at[i])
        load(("step", i), 10 + i, wstep.at[:, pl.ds(at, half)], wstep_v.at[i])
        load(("scan", i), 12 + i, wscan.at[pl.ds(at, half)], wscan_v.at[i])
    for i, at in enumerate(places):
        load(("out", i), 14 + i, wout.at[:, pl.ds(at, half)], wout_v.at[i])

    barrier = pltpu.get_barrier_semaphore()
    pl.semaphore_signal(barrier, inc=1, device_id={"chan": partner}, device_id_type=MESH)

    def greet(k, carry):
        pl.semaphore_signal(
            barrier, inc=1, device_id={"seq": lax.rem(me + k, n)}, device_id_type=MESH
        )
        return carry

    lax.fori_loop(1, n, greet, 0)
    pl.semaphore_wait(barrier, n)

    swap = pltpu.make_async_remote_copy(
        src_ref=stream,
        dst_ref=other_stream,
        send_sem=xs_send,
        recv_sem=xs_recv,
        device_id={"chan": partner},
        device_id_type=MESH,
    )
    swap.start()

    ids_row = ids[...]
    onehot_t = (lax.broadcasted_iota(jnp.int32, (128, rows), 0) == ids_row).astype(F32)
    onehot = onehot_t.T.astype(BF16)
    loads["emb", 0].wait()
    hid[0] = (stream[...].astype(F32) + mm(onehot, emb_v[0])).astype(BF16)
    loads["emb", 1].wait()
    added = mm(onehot, emb_v[1])
    swap.wait()
    hid[1] = (other_stream[...].astype(F32) + added).astype(BF16)

    limit = glen[0]
    key_rows = me * rows + lax.broadcasted_iota(jnp.int32, (rows, HEAD_DIM), 0)
    key_ok = key_rows < limit

    def project(part):
        loads["att", part, 0].wait()
        loads["att", part, 1].wait()
        return mm(hid[0], watt_v[part, 0]) + mm(hid[1], watt_v[part, 1])

    keys = project(1)
    for h in range(heads):
        kvsend[h, 0] = normed(keys[:, h * HEAD_DIM : (h + 1) * HEAD_DIM]).astype(BF16)
    values = project(2)
    for h in range(heads):
        kvsend[h, 1] = jnp.where(
            key_ok, values[:, h * HEAD_DIM : (h + 1) * HEAD_DIM], 0.0
        ).astype(BF16)

    def kv_copy(k):
        to = lax.rem(me + k, n)
        return pltpu.make_async_remote_copy(
            src_ref=kvsend.at[lax.rem(to, heads)],
            dst_ref=kvrecv.at[me],
            send_sem=kv_ss.at[k],
            recv_sem=kv_rs.at[k],
            device_id={"seq": to},
            device_id_type=MESH,
        )

    def kv_start(k, carry):
        kv_copy(k).start()
        return carry

    lax.fori_loop(1, n, kv_start, 0)
    kvrecv[me] = kvsend[member]

    queries = project(0)
    for h in range(heads):
        qsend[h] = normed(queries[:, h * HEAD_DIM : (h + 1) * HEAD_DIM]).astype(BF16)

    def q_copy(k):
        to = lax.rem(member + k, heads)
        return pltpu.make_async_remote_copy(
            src_ref=qsend.at[to],
            dst_ref=qrecv.at[member],
            send_sem=q_ss.at[k],
            recv_sem=q_rs.at[k],
            device_id={"seq": base + to},
            device_id_type=MESH,
        )

    for k in range(1, heads):
        q_copy(k).start()
    qrecv[member] = qsend[member]

    loads["state", 0].wait()
    loads["state", 1].wait()
    state = silu(mm(hid[0], wstate_v[0]) + mm(hid[1], wstate_v[1])).astype(BF16).astype(F32)
    turned = jnp.concatenate([state[:, STATE:], state[:, :STATE]], axis=1)
    low_lane = lax.broadcasted_iota(jnp.int32, (rows, 2 * STATE), 1) < STATE
    bb = jnp.where(low_lane, state, turned)
    cc = jnp.where(low_lane, turned, state)
    bb_t = bb.T
    low_row = lax.broadcasted_iota(jnp.int32, (2 * STATE, rows), 0) < STATE

    loads["step", 0].wait()
    loads["step", 1].wait()
    raw = mm_nt(wstep_v[0], hid[0]) + mm_nt(wstep_v[1], hid[1])
    step_rows = raw.shape[0]
    head_row = lax.broadcasted_iota(jnp.int32, (step_rows, rows), 0)
    bias_full = jnp.zeros((step_rows, rows), F32)
    speed_full = jnp.zeros((step_rows, rows), F32)
    for h in range(heads):
        bias_full = jnp.where(head_row == h, bias[h], bias_full)
        speed_full = jnp.where(head_row == h, speed[h], speed_full)
    shifted = raw + bias_full
    steps = jnp.maximum(shifted, 0.0) + jnp.log1p(jnp.exp(-jnp.abs(shifted)))
    place_row = me * rows + lax.broadcasted_iota(jnp.int32, (step_rows, rows), 1)
    ok_row = place_row < limit
    spike = jnp.where(jnp.broadcast_to(ids_row, (step_rows, rows)) == UNCLEAR, SPIKE, 0.0)
    decay = jnp.where(ok_row, spike - speed_full * steps, 0.0)
    used = jnp.where(ok_row, steps, 0.0)
    t_at = lax.broadcasted_iota(jnp.int32, (rows, rows), 0)
    s_at = lax.broadcasted_iota(jnp.int32, (rows, rows), 1)
    forward = exact_mm(decay, (t_at <= s_at).astype(F32).astype(BF16))
    backward = exact_mm(decay, (t_at >= s_at).astype(F32).astype(BF16))
    total = forward[:, rows - 1 : rows]
    first = backward[:, 0:1]
    weight_f = jnp.exp(jnp.minimum(total - forward, 0.0)) * used
    weight_r = jnp.exp(jnp.minimum(first - backward, 0.0)) * used
    passing = jnp.exp(total)
    columns = jnp.concatenate(
        [forward, backward, jnp.zeros((128 - 2 * step_rows, rows), F32)], axis=0
    ).T

    loads["scan", 0].wait()
    loads["scan", 1].wait()
    x_v[...] = silu(mm(hid[0], wscan_v[0]) + mm(hid[1], wscan_v[1])).astype(BF16)

    for h in range(heads):
        lanes = slice(h * HEAD_DIM, (h + 1) * HEAD_DIM)
        scaled = bb_t * jnp.where(low_row, weight_f[h : h + 1], weight_r[h : h + 1])
        ends = mm(scaled.astype(BF16), x_v[:, lanes])
        ends_b = ends.astype(BF16)
        head_pass = jnp.broadcast_to(passing[h : h + 1], (16, HEAD_DIM))
        high = head_pass.astype(BF16)
        low = (head_pass - high.astype(F32)).astype(BF16)
        for piece in range(HEAD_DIM // rpd):
            j = h * (HEAD_DIM // rpd) + piece
            endsend[j, 0:rpd] = ends_b[piece * rpd : (piece + 1) * rpd]
            endsend[j, rpd : rpd + 16] = high
            endsend[j, rpd + 16 : rpd + 32] = low

    def end_copy(k):
        to = lax.rem(me + k, n)
        return pltpu.make_async_remote_copy(
            src_ref=endsend.at[to],
            dst_ref=endrecv.at[me],
            send_sem=en_ss.at[k],
            recv_sem=en_rs.at[k],
            device_id={"seq": to},
            device_id_type=MESH,
        )

    def end_start(k, carry):
        end_copy(k).start()
        return carry

    lax.fori_loop(1, n, end_start, 0)
    endrecv[me] = endsend[me]

    pairing = mm_nt(jnp.where(low_lane, cc, 0.0).astype(BF16), bb.astype(BF16))
    pairing = jnp.where(t_at == s_at, 2.0 * pairing, pairing)
    for h in range(heads):
        lanes = slice(h * HEAD_DIM, (h + 1) * HEAD_DIM)
        gap = jnp.where(
            t_at >= s_at,
            columns[:, h : h + 1] - forward[h : h + 1],
            columns[:, step_rows + h : step_rows + h + 1] - backward[h : h + 1],
        )
        mixing = pairing * jnp.exp(jnp.minimum(gap, 0.0)) * used[h : h + 1]
        loc_v[:, lanes] = mm(mixing.astype(BF16), x_v[:, lanes])

    for k in range(1, heads):
        q_copy(k).wait()
    acc[...] = jnp.zeros_like(acc)
    scale = 2.0 / math.sqrt(HEAD_DIM) * math.log2(math.e)
    lane_rows = lax.broadcasted_iota(jnp.int32, (rows, HEAD_DIM), 0)

    def absorb(source):
        ones = (source * rows + lane_rows < limit).astype(F32).astype(BF16)
        key = kvrecv[source, 0]
        value = jnp.concatenate([kvrecv[source, 1], ones], axis=1)
        for m in range(heads):
            weights = jnp.exp2(mm_nt(qrecv[m], key) * scale).astype(BF16)
            acc[m] += mm(weights, value)

    absorb(me)

    def attend(k, carry):
        kv_copy(k).wait()
        absorb(lax.rem(me - k + n, n))
        return carry

    lax.fori_loop(1, n, attend, 0)
    for m in range(heads):
        attsend[m] = normed(acc[m, :, :HEAD_DIM] / acc[m, :, HEAD_DIM:]).astype(BF16)

    def att_copy(k):
        to = lax.rem(member + k, heads)
        return pltpu.make_async_remote_copy(
            src_ref=attsend.at[to],
            dst_ref=attrecv.at[member],
            send_sem=at_ss.at[k],
            recv_sem=at_rs.at[k],
            device_id={"seq": base + to},
            device_id_type=MESH,
        )

    for k in range(1, heads):
        att_copy(k).start()
    attrecv[member] = attsend[member]

    def end_wait(k, carry):
        end_copy(k).wait()
        return carry

    lax.fori_loop(1, n, end_wait, 0)
    reverse = lax.rem(me * rpd // STATE, 2)

    def element(t):
        at = t + reverse * (n - 1 - 2 * t)
        message = endrecv[at].astype(F32)
        factor = message[rpd : rpd + 1] + message[rpd + 16 : rpd + 17]
        return at, message[:rpd], factor

    def lap(t, carry):
        held, product = carry
        _, finish, factor = element(t)
        return factor * held + finish, product * factor

    held, product = lax.fori_loop(
        0, n, lap, (jnp.zeros((rpd, HEAD_DIM), F32), jnp.ones((1, HEAD_DIM), F32))
    )

    def enter(t, held):
        at, finish, factor = element(t)
        entsend[at] = held.astype(BF16)
        return factor * held + finish

    lax.fori_loop(0, n, enter, held / (1.0 - product))

    def ent_copy(k):
        to = lax.rem(me + k, n)
        return pltpu.make_async_remote_copy(
            src_ref=entsend.at[to],
            dst_ref=entrecv.at[me],
            send_sem=er_ss.at[k],
            recv_sem=er_rs.at[k],
            device_id={"seq": to},
            device_id_type=MESH,
        )

    def ent_start(k, carry):
        ent_copy(k).start()
        return carry

    lax.fori_loop(1, n, ent_start, 0)
    entrecv[me] = entsend[me]

    def ent_wait(k, carry):
        ent_copy(k).wait()
        return carry

    lax.fori_loop(1, n, ent_wait, 0)
    per_head = HEAD_DIM // rpd
    scanned = []
    for h in range(heads):
        lanes = slice(h * HEAD_DIM, (h + 1) * HEAD_DIM)
        reading = cc * jnp.exp(
            jnp.where(
                low_lane,
                columns[:, h : h + 1],
                columns[:, step_rows + h : step_rows + h + 1],
            )
        )
        entering = entrecv[h * per_head : (h + 1) * per_head].reshape(HEAD_DIM, HEAD_DIM)
        loc_v[:, lanes] = normed(loc_v[:, lanes] + mm(reading.astype(BF16), entering)) * sgain[
            :, lanes
        ]

    for k in range(1, heads):
        att_copy(k).wait()
    for h in range(heads):
        lanes = slice(h * HEAD_DIM, (h + 1) * HEAD_DIM)
        comb_v[:, lanes] = (
            again[:, lanes] * attrecv[h].astype(F32) + loc_v[:, lanes]
        ).astype(BF16)

    loads["out", 0].wait()
    loads["out", 1].wait()
    combined = comb_v[...]
    pieces = psend.shape[0]
    width = half // pieces
    shares = []
    for p in range(pieces):
        psend[p] = mm(combined, wout_v[1, :, p * width : (p + 1) * width])
        share = pltpu.make_async_remote_copy(
            src_ref=psend.at[p],
            dst_ref=precv.at[p],
            send_sem=ps_ss.at[p],
            recv_sem=ps_rs.at[p],
            device_id={"chan": partner},
            device_id_type=MESH,
        )
        share.start()
        shares.append(share)
    for p in range(pieces):
        lanes = slice(p * width, (p + 1) * width)
        mine = stream[:, lanes].astype(F32) + mm(combined, wout_v[0, :, lanes])
        shares[p].wait()
        out[:, lanes] = (mine + precv[p]).astype(BF16)


def local(
    n,
    stream,
    ids,
    genome_length,
    embedding,
    attention_in,
    scan_input,
    state_maps,
    step_weight,
    step_bias,
    head_decay_speed,
    attention_gain,
    scan_gain,
    out_weight,
):
    rows, half = stream.shape
    heads = step_weight.shape[1]
    span = heads * HEAD_DIM
    rpd = span // n
    step_rows = 16
    pieces = 4
    vmem = pl.BlockSpec(memory_space=pltpu.VMEM)
    smem = pl.BlockSpec(memory_space=pltpu.SMEM)
    anywhere = pl.BlockSpec(memory_space=pl.ANY)
    dma = pltpu.SemaphoreType.DMA
    V = pltpu.VMEM
    return pl.pallas_call(
        functools.partial(kernel, n),
        out_shape=jax.ShapeDtypeStruct((rows, half), BF16),
        in_specs=[
            vmem,
            vmem,
            smem,
            anywhere,
            anywhere,
            anywhere,
            anywhere,
            anywhere,
            smem,
            smem,
            vmem,
            vmem,
            anywhere,
        ],
        out_specs=vmem,
        scratch_shapes=[
            V((2, 128, half), BF16),
            V((3, 2, half, span), BF16),
            V((2, half, span), BF16),
            V((2, half, 2 * STATE), BF16),
            V((2, step_rows, half), BF16),
            V((2, span, half), BF16),
            V((rows, half), BF16),
            V((2, rows, half), BF16),
            V((heads, 2, rows, HEAD_DIM), BF16),
            V((n, 2, rows, HEAD_DIM), BF16),
            V((heads, rows, HEAD_DIM), BF16),
            V((heads, rows, HEAD_DIM), BF16),
            V((heads, rows, 2 * HEAD_DIM), F32),
            V((heads, rows, HEAD_DIM), BF16),
            V((heads, rows, HEAD_DIM), BF16),
            V((n, rpd + 32, HEAD_DIM), BF16),
            V((n, rpd + 32, HEAD_DIM), BF16),
            V((n, rpd, HEAD_DIM), BF16),
            V((n, rpd, HEAD_DIM), BF16),
            V((rows, span), BF16),
            V((rows, span), F32),
            V((rows, span), BF16),
            V((pieces, rows, half // pieces), F32),
            V((pieces, rows, half // pieces), F32),
            dma((16,)),
            dma,
            dma,
            dma((n,)),
            dma((n,)),
            dma((heads,)),
            dma((heads,)),
            dma((heads,)),
            dma((heads,)),
            dma((n,)),
            dma((n,)),
            dma((n,)),
            dma((n,)),
            dma((pieces,)),
            dma((pieces,)),
        ],
        compiler_params=pltpu.CompilerParams(
            collective_id=0, has_side_effects=True, vmem_limit_bytes=52 * 1024 * 1024
        ),
    )(
        stream,
        ids.reshape(1, rows),
        genome_length,
        embedding,
        jnp.transpose(attention_in, (1, 0, 2)),
        scan_input,
        state_maps,
        jnp.pad(step_weight.T, ((0, step_rows - heads), (0, 0))),
        step_bias,
        head_decay_speed,
        attention_gain.reshape(1, span),
        scan_gain.reshape(1, span),
        out_weight,
    )


def solution(mesh):
    placed = (
        P(("groups", "seq"), "chan"),
        P(("groups", "seq")),
        P("groups"),
        P(),
        P(None, None, "chan"),
        P(None, "chan"),
        P(None, "chan"),
        P(None, "chan"),
        P("chan"),
        P("chan"),
        P("chan"),
        P("chan"),
        P("chan", None),
    )
    return jax.shard_map(
        functools.partial(local, mesh.shape["seq"]),
        mesh=mesh,
        in_specs=placed,
        out_specs=P(("groups", "seq"), "chan"),
        check_vma=False,
    )
```

```python
import functools
import math

import jax
import jax.numpy as jnp
from jax import lax
from jax.experimental import pallas as pl
from jax.experimental.pallas import tpu as pltpu
from jax.sharding import PartitionSpec as P

HEAD_DIM = 128
STATE = 64
EPS = 1e-06
SPIKE = math.log(0.7)
UNCLEAR = 11
F32 = jnp.float32
BF16 = jnp.bfloat16
MESH = pl.DeviceIdType.MESH


def mm(a, b):
    return lax.dot_general(a, b, (((1,), (0,)), ((), ())), preferred_element_type=F32)


def mm_nt(a, b):
    return lax.dot_general(a, b, (((1,), (1,)), ((), ())), preferred_element_type=F32)


def normed(v):
    return v * lax.rsqrt(jnp.mean(v * v, axis=-1, keepdims=True) + EPS)


def silu(v):
    return v / (1.0 + jnp.exp(-v))


def exact_mm(a, b):
    first = a.astype(BF16)
    rest = a - first.astype(F32)
    second = rest.astype(BF16)
    third = (rest - second.astype(F32)).astype(BF16)
    return mm(first, b) + (mm(second, b) + mm(third, b))


def halves(v):
    high = v.astype(BF16)
    return jnp.concatenate([high.astype(F32), v - high.astype(F32)], axis=0).astype(BF16)


def kernel(
    n,
    stream_hbm,
    ids_hbm,
    glen_hbm,
    emb,
    watt,
    wscan,
    wstate,
    wstep,
    bias_hbm,
    speed_hbm,
    again_hbm,
    sgain_hbm,
    wout,
    out,
    stream,
    ids,
    glen,
    bias,
    speed,
    again,
    sgain,
    emb_v,
    watt_v,
    wscan_v,
    wstate_v,
    wstep_v,
    wout_v,
    other_stream,
    hid,
    kvsend,
    kvrecv,
    qsend,
    qrecv,
    acc,
    attsend,
    attrecv,
    endsend,
    endrecv,
    runsend,
    runrecv,
    entsend,
    entrecv,
    part_k,
    part_v,
    part_q,
    part_x,
    hid_add,
    x_v,
    loc_v,
    comb_v,
    psend,
    precv,
    wsem,
    xs_send,
    xs_recv,
    kv_ss,
    kv_rs,
    q_ss,
    q_rs,
    at_ss,
    at_rs,
    en_ss,
    en_rs,
    ru_ss,
    ru_rs,
    er_ss,
    er_rs,
    ps_ss,
    ps_rs,
):
    rows, half = stream.shape
    heads = kvsend.shape[0]
    me = lax.axis_index("seq")
    chan = lax.axis_index("chan")
    partner = 1 - chan
    member = lax.rem(me, heads)
    base = me - member
    span = heads * HEAD_DIM

    own_at = pl.multiple_of(chan * half, half)
    other_at = pl.multiple_of(partner * half, half)
    places = (own_at, other_at)

    barrier = pltpu.get_barrier_semaphore()
    pl.semaphore_signal(barrier, inc=1, device_id={"chan": partner}, device_id_type=MESH)

    def greet(k, carry):
        pl.semaphore_signal(
            barrier, inc=1, device_id={"seq": lax.rem(me + k, n)}, device_id_type=MESH
        )
        return carry

    lax.fori_loop(1, n, greet, 0)

    loads = {}

    def load(name, index, src, dst):
        copy = pltpu.make_async_copy(src, dst, wsem.at[index])
        copy.start()
        loads[name] = copy

    load("ids", 16, ids_hbm, ids)
    load("stream", 17, stream_hbm, stream)
    load("glen", 18, glen_hbm, glen)
    load("bias", 19, bias_hbm, bias)
    load("speed", 20, speed_hbm, speed)
    emb_v[...] = jnp.zeros_like(emb_v)
    vocab = emb.shape[0]
    for i, at in enumerate(places):
        load(("emb", i), i, emb.at[:, pl.ds(at, half)], emb_v.at[i, pl.ds(0, vocab)])
    for j, part in enumerate((1, 2, 0)):
        for i, at in enumerate(places):
            load(
                ("att", part, i),
                2 + 2 * j + i,
                watt.at[part, pl.ds(at, half)],
                watt_v.at[part, i],
            )
    for i, at in enumerate(places):
        load(("state", i), 8 + i, wstate.at[pl.ds(at, half)], wstate_v.at[i])
        load(("step", i), 10 + i, wstep.at[:, pl.ds(at, half)], wstep_v.at[i])
        load(("scan", i), 12 + i, wscan.at[pl.ds(at, half)], wscan_v.at[i])
    for i, at in enumerate(places):
        load(("out", i), 14 + i, wout.at[:, pl.ds(at, half)], wout_v.at[i])
    load("again", 21, again_hbm, again)
    load("sgain", 22, sgain_hbm, sgain)


    loads["ids"].wait()
    ids_row = ids[...]
    onehot_t = (lax.broadcasted_iota(jnp.int32, (128, rows), 0) == ids_row).astype(F32)
    onehot = onehot_t.T.astype(BF16)
    loads["emb", 0].wait()
    loads["stream"].wait()
    hid[0] = (stream[...].astype(F32) + mm(onehot, emb_v[0])).astype(BF16)
    loads["glen"].wait()
    limit = glen[0]
    key_rows = me * rows + lax.broadcasted_iota(jnp.int32, (rows, HEAD_DIM), 0)
    key_ok = key_rows < limit

    def project(part, i):
        loads["att", part, i].wait()
        return mm(hid[i], watt_v[part, i])

    part_k[...] = project(1, 0)
    part_v[...] = project(2, 0)
    pl.semaphore_wait(barrier, n)
    swap = pltpu.make_async_remote_copy(
        src_ref=stream_hbm,
        dst_ref=other_stream,
        send_sem=xs_send,
        recv_sem=xs_recv,
        device_id={"chan": partner},
        device_id_type=MESH,
    )
    swap.start()
    loads["emb", 1].wait()
    hid_add[...] = mm(onehot, emb_v[1])
    part_q[...] = project(0, 0)
    loads["scan", 0].wait()
    part_x[...] = mm(hid[0], wscan_v[0])
    swap.wait()
    hid[1] = (other_stream[...].astype(F32) + hid_add[...]).astype(BF16)

    group_count = n // heads
    group = lax.div(me, heads)

    def routed(t, sign):
        far = group_count - 1 - lax.div(t, heads)
        near = heads - 1 - lax.rem(t, heads)
        to_group = lax.rem(group + sign * far + group_count, group_count)
        return to_group * heads + lax.rem(member + sign * near + heads, heads)

    def kv_copy(j, t):
        to = routed(t, 1)
        return pltpu.make_async_remote_copy(
            src_ref=kvsend.at[lax.rem(to, heads), j],
            dst_ref=kvrecv.at[me, j],
            send_sem=kv_ss.at[j, t],
            recv_sem=kv_rs.at[j, t],
            device_id={"seq": to},
            device_id_type=MESH,
        )

    def k_start(t, carry):
        kv_copy(0, t).start()
        return carry

    def v_start(t, carry):
        kv_copy(1, t).start()
        return carry

    keys = part_k[...] + project(1, 1)
    for h in range(heads):
        kvsend[h, 0] = normed(keys[:, h * HEAD_DIM : (h + 1) * HEAD_DIM]).astype(BF16)
    lax.fori_loop(0, n - 1, k_start, 0)
    values = part_v[...] + project(2, 1)
    for h in range(heads):
        kvsend[h, 1] = jnp.where(
            key_ok, values[:, h * HEAD_DIM : (h + 1) * HEAD_DIM], 0.0
        ).astype(BF16)
    lax.fori_loop(0, n - 1, v_start, 0)
    kvrecv[me] = kvsend[member]

    queries = part_q[...] + project(0, 1)
    for h in range(heads):
        qsend[h] = normed(queries[:, h * HEAD_DIM : (h + 1) * HEAD_DIM]).astype(BF16)

    def q_copy(k):
        to = lax.rem(member + k, heads)
        return pltpu.make_async_remote_copy(
            src_ref=qsend.at[to],
            dst_ref=qrecv.at[member],
            send_sem=q_ss.at[k],
            recv_sem=q_rs.at[k],
            device_id={"seq": base + to},
            device_id_type=MESH,
        )

    for k in range(1, heads):
        q_copy(k).start()
    qrecv[member] = qsend[member]

    loads["state", 0].wait()
    loads["state", 1].wait()
    state = silu(mm(hid[0], wstate_v[0]) + mm(hid[1], wstate_v[1])).astype(BF16).astype(F32)
    turned = jnp.concatenate([state[:, STATE:], state[:, :STATE]], axis=1)
    low_lane = lax.broadcasted_iota(jnp.int32, (rows, 2 * STATE), 1) < STATE
    bb = jnp.where(low_lane, state, turned)
    cc = jnp.where(low_lane, turned, state)
    bb_t = bb.T
    low_row = lax.broadcasted_iota(jnp.int32, (2 * STATE, rows), 0) < STATE

    loads["bias"].wait()
    loads["speed"].wait()
    loads["step", 0].wait()
    loads["step", 1].wait()
    raw = mm_nt(wstep_v[0], hid[0]) + mm_nt(wstep_v[1], hid[1])
    step_rows = 8
    raw = jnp.concatenate([raw, jnp.zeros((step_rows - heads, rows), F32)], axis=0)
    head_row = lax.broadcasted_iota(jnp.int32, (step_rows, rows), 0)
    bias_full = jnp.zeros((step_rows, rows), F32)
    speed_full = jnp.zeros((step_rows, rows), F32)
    for h in range(heads):
        bias_full = jnp.where(head_row == h, bias[h], bias_full)
        speed_full = jnp.where(head_row == h, speed[h], speed_full)
    shifted = raw + bias_full
    steps = jnp.maximum(shifted, 0.0) + jnp.log1p(jnp.exp(-jnp.abs(shifted)))
    place_row = me * rows + lax.broadcasted_iota(jnp.int32, (step_rows, rows), 1)
    ok_row = place_row < limit
    spike = jnp.where(jnp.broadcast_to(ids_row, (step_rows, rows)) == UNCLEAR, SPIKE, 0.0)
    decay = jnp.where(ok_row, spike - speed_full * steps, 0.0)
    used = jnp.where(ok_row, steps, 0.0)
    t_at = lax.broadcasted_iota(jnp.int32, (rows, rows), 0)
    s_at = lax.broadcasted_iota(jnp.int32, (rows, rows), 1)
    forward = exact_mm(decay, (t_at <= s_at).astype(F32).astype(BF16))
    backward = exact_mm(decay, (t_at >= s_at).astype(F32).astype(BF16))
    total = forward[:, rows - 1 : rows]
    first = backward[:, 0:1]
    weight_f = jnp.exp(jnp.minimum(total - forward, 0.0)) * used
    weight_r = jnp.exp(jnp.minimum(first - backward, 0.0)) * used
    passing = jnp.exp(total)
    columns = jnp.concatenate(
        [forward, backward, jnp.zeros((128 - 2 * step_rows, rows), F32)], axis=0
    ).T

    loads["scan", 1].wait()
    x_v[...] = silu(part_x[...] + mm(hid[1], wscan_v[1])).astype(BF16)

    for h in range(heads):
        lanes = slice(h * HEAD_DIM, (h + 1) * HEAD_DIM)
        scaled = bb_t * jnp.where(low_row, weight_f[h : h + 1], weight_r[h : h + 1])
        ends = mm(scaled.astype(BF16), x_v[:, lanes])
        endsend[h, 0:HEAD_DIM] = ends.astype(BF16)
        endsend[h, HEAD_DIM : HEAD_DIM + 16] = halves(
            jnp.broadcast_to(passing[h : h + 1], (8, HEAD_DIM))
        )

    def end_copy(k):
        to = lax.rem(member + k, heads)
        return pltpu.make_async_remote_copy(
            src_ref=endsend.at[to],
            dst_ref=endrecv.at[member],
            send_sem=en_ss.at[k],
            recv_sem=en_rs.at[k],
            device_id={"seq": base + to},
            device_id_type=MESH,
        )

    for k in range(1, heads):
        end_copy(k).start()
    endrecv[member] = endsend[member]

    loads["again"].wait()
    loads["sgain"].wait()
    pairing = mm_nt(jnp.where(low_lane, cc, 0.0).astype(BF16), bb.astype(BF16))
    pairing = jnp.where(t_at == s_at, 2.0 * pairing, pairing)
    for h in range(heads):
        lanes = slice(h * HEAD_DIM, (h + 1) * HEAD_DIM)
        gap = jnp.where(
            t_at >= s_at,
            columns[:, h : h + 1] - forward[h : h + 1],
            columns[:, step_rows + h : step_rows + h + 1] - backward[h : h + 1],
        )
        mixing = pairing * jnp.exp(jnp.minimum(gap, 0.0)) * used[h : h + 1]
        loc_v[:, lanes] = mm(mixing.astype(BF16), x_v[:, lanes])

    for k in range(1, heads):
        q_copy(k).wait()
    acc[...] = jnp.zeros_like(acc)
    scale = 2.0 / math.sqrt(HEAD_DIM) * math.log2(math.e)
    lane_rows = lax.broadcasted_iota(jnp.int32, (rows, HEAD_DIM), 0)

    def absorb(source):
        ones = (source * rows + lane_rows < limit).astype(F32).astype(BF16)
        key = kvrecv[source, 0]
        value = jnp.concatenate([kvrecv[source, 1], ones], axis=1)
        for m in range(heads):
            weights = jnp.exp2(mm_nt(qrecv[m], key) * scale).astype(BF16)
            acc[m] += mm(weights, value)

    absorb(me)

    def attend(t, carry):
        kv_copy(0, t).wait()
        kv_copy(1, t).wait()
        absorb(routed(t, -1))
        return carry

    def message(ref, i):
        whole = ref[i].astype(F32)
        factor = whole[HEAD_DIM : HEAD_DIM + 1] + whole[HEAD_DIM + 8 : HEAD_DIM + 9]
        return whole[:STATE], whole[STATE:HEAD_DIM], factor

    def run_copy(k):
        return pltpu.make_async_remote_copy(
            src_ref=runsend,
            dst_ref=runrecv.at[group],
            send_sem=ru_ss.at[k],
            recv_sem=ru_rs.at[k],
            device_id={"seq": lax.rem(group + k, group_count) * heads + member},
            device_id_type=MESH,
        )

    def ent_copy(k):
        to = lax.rem(member + k, heads)
        return pltpu.make_async_remote_copy(
            src_ref=entsend.at[to],
            dst_ref=entrecv.at[member],
            send_sem=er_ss.at[k],
            recv_sem=er_rs.at[k],
            device_id={"seq": base + to},
            device_id_type=MESH,
        )

    nothing = jnp.zeros((STATE, HEAD_DIM), F32)
    near_end = 3 * n // 8
    far_end = 5 * n // 8
    lax.fori_loop(0, near_end, attend, 0)

    for k in range(1, heads):
        end_copy(k).wait()
    run_f, run_r = nothing, nothing
    run_pass = jnp.ones((1, HEAD_DIM), F32)
    for b in range(heads):
        end_f, _, factor = message(endrecv, b)
        run_f = factor * run_f + end_f
        run_pass = run_pass * factor
        _, end_r, factor = message(endrecv, heads - 1 - b)
        run_r = factor * run_r + end_r
    runsend[0:STATE] = run_f.astype(BF16)
    runsend[STATE:HEAD_DIM] = run_r.astype(BF16)
    runsend[HEAD_DIM : HEAD_DIM + 16] = halves(jnp.broadcast_to(run_pass, (8, HEAD_DIM)))

    def run_start(k, carry):
        run_copy(k).start()
        return carry

    def run_wait(k, carry):
        run_copy(k).wait()
        return carry

    lax.fori_loop(1, group_count, run_start, 0)
    runrecv[group] = runsend[...]
    lax.fori_loop(near_end, far_end, attend, 0)

    lax.fori_loop(1, group_count, run_wait, 0)

    def lap(t, carry):
        enter_f, enter_r, product = carry
        end_f, _, factor = message(runrecv, lax.rem(group + t, group_count))
        _, end_r, factor_r = message(runrecv, lax.rem(group - t + group_count, group_count))
        return factor * enter_f + end_f, factor_r * enter_r + end_r, product * factor

    enter_f, enter_r, product = lax.fori_loop(
        0, group_count, lap, (nothing, nothing, jnp.ones((1, HEAD_DIM), F32))
    )
    enter_f = enter_f / (1.0 - product)
    enter_r = enter_r / (1.0 - product)
    for b in range(heads):
        entsend[b, 0:STATE] = enter_f.astype(BF16)
        end_f, _, factor = message(endrecv, b)
        enter_f = factor * enter_f + end_f
        back = heads - 1 - b
        entsend[back, STATE:HEAD_DIM] = enter_r.astype(BF16)
        _, end_r, factor = message(endrecv, back)
        enter_r = factor * enter_r + end_r
    for k in range(1, heads):
        ent_copy(k).start()
    entrecv[member] = entsend[member]
    lax.fori_loop(far_end, n - 1, attend, 0)
    for m in range(heads):
        attsend[m] = normed(acc[m, :, :HEAD_DIM] / acc[m, :, HEAD_DIM:]).astype(BF16)

    def att_copy(k):
        to = lax.rem(member + k, heads)
        return pltpu.make_async_remote_copy(
            src_ref=attsend.at[to],
            dst_ref=attrecv.at[member],
            send_sem=at_ss.at[k],
            recv_sem=at_rs.at[k],
            device_id={"seq": base + to},
            device_id_type=MESH,
        )

    for k in range(1, heads):
        att_copy(k).start()
    attrecv[member] = attsend[member]

    for k in range(1, heads):
        ent_copy(k).wait()
    for h in range(heads):
        lanes = slice(h * HEAD_DIM, (h + 1) * HEAD_DIM)
        reading = cc * jnp.exp(
            jnp.where(
                low_lane,
                columns[:, h : h + 1],
                columns[:, step_rows + h : step_rows + h + 1],
            )
        )
        entering = entrecv[h]
        loc_v[:, lanes] = normed(loc_v[:, lanes] + mm(reading.astype(BF16), entering)) * sgain[
            :, lanes
        ]

    for k in range(1, heads):
        att_copy(k).wait()
    for h in range(heads):
        lanes = slice(h * HEAD_DIM, (h + 1) * HEAD_DIM)
        comb_v[:, lanes] = (
            again[:, lanes] * attrecv[h].astype(F32) + loc_v[:, lanes]
        ).astype(BF16)

    loads["out", 0].wait()
    loads["out", 1].wait()
    combined = comb_v[...]
    pieces = psend.shape[0]
    width = half // pieces
    shares = []
    for p in range(pieces):
        psend[p] = mm(combined, wout_v[1, :, p * width : (p + 1) * width])
        share = pltpu.make_async_remote_copy(
            src_ref=psend.at[p],
            dst_ref=precv.at[p],
            send_sem=ps_ss.at[p],
            recv_sem=ps_rs.at[p],
            device_id={"chan": partner},
            device_id_type=MESH,
        )
        share.start()
        shares.append(share)
    for p in range(pieces):
        lanes = slice(p * width, (p + 1) * width)
        mine = stream[:, lanes].astype(F32) + mm(combined, wout_v[0, :, lanes])
        shares[p].wait()
        out[:, lanes] = (mine + precv[p]).astype(BF16)


def local(
    n,
    stream,
    ids,
    genome_length,
    embedding,
    attention_in,
    scan_input,
    state_maps,
    step_weight,
    step_bias,
    head_decay_speed,
    attention_gain,
    scan_gain,
    out_weight,
):
    rows, half = stream.shape
    heads = step_weight.shape[1]
    span = heads * HEAD_DIM
    groups = n // heads
    pieces = 4
    vmem = pl.BlockSpec(memory_space=pltpu.VMEM)
    anywhere = pl.BlockSpec(memory_space=pltpu.HBM)
    dma = pltpu.SemaphoreType.DMA
    V = pltpu.VMEM
    return pl.pallas_call(
        functools.partial(kernel, n),
        out_shape=jax.ShapeDtypeStruct((rows, half), BF16),
        in_specs=[anywhere] * 13,
        out_specs=vmem,
        scratch_shapes=[
            V((rows, half), BF16),
            V((1, rows), jnp.int32),
            pltpu.SMEM((1,), jnp.int32),
            pltpu.SMEM((heads,), F32),
            pltpu.SMEM((heads,), F32),
            V((1, span), F32),
            V((1, span), F32),
            V((2, 128, half), BF16),
            V((3, 2, half, span), BF16),
            V((2, half, span), BF16),
            V((2, half, 2 * STATE), BF16),
            V((2, heads, half), BF16),
            V((2, span, half), BF16),
            V((rows, half), BF16),
            V((2, rows, half), BF16),
            V((heads, 2, rows, HEAD_DIM), BF16),
            V((n, 2, rows, HEAD_DIM), BF16),
            V((heads, rows, HEAD_DIM), BF16),
            V((heads, rows, HEAD_DIM), BF16),
            V((heads, rows, 2 * HEAD_DIM), F32),
            V((heads, rows, HEAD_DIM), BF16),
            V((heads, rows, HEAD_DIM), BF16),
            V((heads, HEAD_DIM + 16, HEAD_DIM), BF16),
            V((heads, HEAD_DIM + 16, HEAD_DIM), BF16),
            V((HEAD_DIM + 16, HEAD_DIM), BF16),
            V((groups, HEAD_DIM + 16, HEAD_DIM), BF16),
            V((heads, HEAD_DIM, HEAD_DIM), BF16),
            V((heads, HEAD_DIM, HEAD_DIM), BF16),
            V((rows, span), F32),
            V((rows, span), F32),
            V((rows, span), F32),
            V((rows, span), F32),
            V((rows, half), F32),
            V((rows, span), BF16),
            V((rows, span), F32),
            V((rows, span), BF16),
            V((pieces, rows, half // pieces), F32),
            V((pieces, rows, half // pieces), F32),
            dma((23,)),
            dma,
            dma,
            dma((2, n)),
            dma((2, n)),
            dma((heads,)),
            dma((heads,)),
            dma((heads,)),
            dma((heads,)),
            dma((heads,)),
            dma((heads,)),
            dma((groups,)),
            dma((groups,)),
            dma((heads,)),
            dma((heads,)),
            dma((pieces,)),
            dma((pieces,)),
        ],
        compiler_params=pltpu.CompilerParams(
            collective_id=0, has_side_effects=True, vmem_limit_bytes=60 * 1024 * 1024
        ),
    )(
        stream,
        ids.reshape(1, rows),
        genome_length,
        embedding,
        jnp.transpose(attention_in, (1, 0, 2)),
        scan_input,
        state_maps,
        step_weight.T,
        step_bias,
        head_decay_speed,
        attention_gain.reshape(1, span),
        scan_gain.reshape(1, span),
        out_weight,
    )


def solution(mesh):
    placed = (
        P(("groups", "seq"), "chan"),
        P(("groups", "seq")),
        P("groups"),
        P(),
        P(None, None, "chan"),
        P(None, "chan"),
        P(None, "chan"),
        P(None, "chan"),
        P("chan"),
        P("chan"),
        P("chan"),
        P("chan"),
        P("chan", None),
    )
    return jax.shard_map(
        functools.partial(local, mesh.shape["seq"]),
        mesh=mesh,
        in_specs=placed,
        out_specs=P(("groups", "seq"), "chan"),
        check_vma=False,
    )
```

```python
import functools
import math

import jax
import jax.numpy as jnp
from jax import lax
from jax.experimental import pallas as pl
from jax.experimental.pallas import tpu as pltpu
from jax.sharding import PartitionSpec as P

HEAD_DIM = 128
STATE = 64
EPS = 1e-06
SPIKE = math.log(0.7)
UNCLEAR = 11
F32 = jnp.float32
BF16 = jnp.bfloat16
MESH = pl.DeviceIdType.MESH


def mm(a, b):
    return lax.dot_general(a, b, (((1,), (0,)), ((), ())), preferred_element_type=F32)


def mm_nt(a, b):
    return lax.dot_general(a, b, (((1,), (1,)), ((), ())), preferred_element_type=F32)


def normed(v):
    return v * lax.rsqrt(jnp.mean(v * v, axis=-1, keepdims=True) + EPS)


def silu(v):
    return v / (1.0 + jnp.exp(-v))


def exact_mm(a, b):
    first = a.astype(BF16)
    rest = a - first.astype(F32)
    second = rest.astype(BF16)
    third = (rest - second.astype(F32)).astype(BF16)
    return mm(first, b) + (mm(second, b) + mm(third, b))


def halves(v):
    high = v.astype(BF16)
    return jnp.concatenate([high.astype(F32), v - high.astype(F32)], axis=0).astype(BF16)


def kernel(
    n,
    stream_hbm,
    ids_hbm,
    glen_hbm,
    emb,
    watt,
    wscan,
    wstate,
    wstep,
    bias_hbm,
    speed_hbm,
    again_hbm,
    sgain_hbm,
    wout,
    out,
    stream,
    ids,
    glen,
    bias,
    speed,
    again,
    sgain,
    emb_v,
    watt_v,
    wscan_v,
    wstate_v,
    wstep_v,
    wout_v,
    other_stream,
    hid,
    kvsend,
    kvrecv,
    qsend,
    qrecv,
    acc,
    attsend,
    attrecv,
    endsend,
    endrecv,
    runsend,
    runrecv,
    entsend,
    entrecv,
    part_k,
    part_v,
    part_q,
    part_x,
    hid_add,
    x_v,
    loc_v,
    comb_v,
    psend,
    precv,
    wsem,
    xs_send,
    xs_recv,
    kv_ss,
    kv_rs,
    q_ss,
    q_rs,
    at_ss,
    at_rs,
    en_ss,
    en_rs,
    ru_ss,
    ru_rs,
    er_ss,
    er_rs,
    ps_ss,
    ps_rs,
):
    rows, half = stream.shape
    heads = kvsend.shape[0]
    me = lax.axis_index("seq")
    chan = lax.axis_index("chan")
    partner = 1 - chan
    member = lax.rem(me, heads)
    base = me - member
    span = heads * HEAD_DIM

    own_at = pl.multiple_of(chan * half, half)
    other_at = pl.multiple_of(partner * half, half)
    places = (own_at, other_at)

    barrier = pltpu.get_barrier_semaphore()
    pl.semaphore_signal(barrier, inc=1, device_id={"chan": partner}, device_id_type=MESH)

    def greet(k, carry):
        pl.semaphore_signal(
            barrier, inc=1, device_id={"seq": lax.rem(me + k, n)}, device_id_type=MESH
        )
        return carry

    lax.fori_loop(1, n, greet, 0)

    loads = {}

    def load(name, index, src, dst):
        copy = pltpu.make_async_copy(src, dst, wsem.at[index])
        copy.start()
        loads[name] = copy

    load("ids", 16, ids_hbm, ids)
    load("stream", 17, stream_hbm, stream)
    load("glen", 18, glen_hbm, glen)
    load("bias", 19, bias_hbm, bias)
    load("speed", 20, speed_hbm, speed)
    emb_v[...] = jnp.zeros_like(emb_v)
    vocab = emb.shape[0]
    for i, at in enumerate(places):
        load(("emb", i), i, emb.at[:, pl.ds(at, half)], emb_v.at[i, pl.ds(0, vocab)])
    for j, part in enumerate((1, 2, 0)):
        for i, at in enumerate(places):
            load(
                ("att", part, i),
                2 + 2 * j + i,
                watt.at[part, pl.ds(at, half)],
                watt_v.at[part, i],
            )
    for i, at in enumerate(places):
        load(("state", i), 8 + i, wstate.at[pl.ds(at, half)], wstate_v.at[i])
        load(("step", i), 10 + i, wstep.at[:, pl.ds(at, half)], wstep_v.at[i])
        load(("scan", i), 12 + i, wscan.at[pl.ds(at, half)], wscan_v.at[i])
    for i, at in enumerate(places):
        load(("out", i), 14 + i, wout.at[:, pl.ds(at, half)], wout_v.at[i])
    load("again", 21, again_hbm, again)
    load("sgain", 22, sgain_hbm, sgain)


    loads["ids"].wait()
    ids_row = ids[...]
    onehot_t = (lax.broadcasted_iota(jnp.int32, (128, rows), 0) == ids_row).astype(F32)
    onehot = onehot_t.T.astype(BF16)
    loads["emb", 0].wait()
    loads["stream"].wait()
    hid[0] = (stream[...].astype(F32) + mm(onehot, emb_v[0])).astype(BF16)
    loads["glen"].wait()
    limit = glen[0]
    key_rows = me * rows + lax.broadcasted_iota(jnp.int32, (rows, HEAD_DIM), 0)
    key_ok = key_rows < limit

    def project(part, i):
        loads["att", part, i].wait()
        return mm(hid[i], watt_v[part, i])

    part_k[...] = project(1, 0)
    part_v[...] = project(2, 0)
    pl.semaphore_wait(barrier, n)
    swap = pltpu.make_async_remote_copy(
        src_ref=stream_hbm,
        dst_ref=other_stream,
        send_sem=xs_send,
        recv_sem=xs_recv,
        device_id={"chan": partner},
        device_id_type=MESH,
    )
    swap.start()
    loads["emb", 1].wait()
    hid_add[...] = mm(onehot, emb_v[1])
    part_q[...] = project(0, 0)
    loads["scan", 0].wait()
    part_x[...] = mm(hid[0], wscan_v[0])
    swap.wait()
    hid[1] = (other_stream[...].astype(F32) + hid_add[...]).astype(BF16)

    group_count = n // heads
    group = lax.div(me, heads)

    def routed(t, sign):
        far = group_count - 1 - lax.rem(t, group_count)
        near = heads - 1 - lax.div(t, group_count)
        to_group = lax.rem(group + sign * far + group_count, group_count)
        return to_group * heads + lax.rem(member + sign * near + heads, heads)

    def kv_copy(j, t):
        to = routed(t, 1)
        return pltpu.make_async_remote_copy(
            src_ref=kvsend.at[lax.rem(to, heads), j],
            dst_ref=kvrecv.at[me, j],
            send_sem=kv_ss.at[j, t],
            recv_sem=kv_rs.at[j, t],
            device_id={"seq": to},
            device_id_type=MESH,
        )

    def k_start(t, carry):
        kv_copy(0, t).start()
        return carry

    def v_start(t, carry):
        kv_copy(1, t).start()
        return carry

    keys = part_k[...] + project(1, 1)
    for h in range(heads):
        kvsend[h, 0] = normed(keys[:, h * HEAD_DIM : (h + 1) * HEAD_DIM]).astype(BF16)
    lax.fori_loop(0, n - 1, k_start, 0)
    values = part_v[...] + project(2, 1)
    for h in range(heads):
        kvsend[h, 1] = jnp.where(
            key_ok, values[:, h * HEAD_DIM : (h + 1) * HEAD_DIM], 0.0
        ).astype(BF16)
    lax.fori_loop(0, n - 1, v_start, 0)
    kvrecv[me] = kvsend[member]

    queries = part_q[...] + project(0, 1)
    for h in range(heads):
        qsend[h] = normed(queries[:, h * HEAD_DIM : (h + 1) * HEAD_DIM]).astype(BF16)

    def q_copy(k):
        to = lax.rem(member + k, heads)
        return pltpu.make_async_remote_copy(
            src_ref=qsend.at[to],
            dst_ref=qrecv.at[member],
            send_sem=q_ss.at[k],
            recv_sem=q_rs.at[k],
            device_id={"seq": base + to},
            device_id_type=MESH,
        )

    for k in range(1, heads):
        q_copy(k).start()
    qrecv[member] = qsend[member]

    loads["state", 0].wait()
    loads["state", 1].wait()
    state = silu(mm(hid[0], wstate_v[0]) + mm(hid[1], wstate_v[1])).astype(BF16).astype(F32)
    turned = jnp.concatenate([state[:, STATE:], state[:, :STATE]], axis=1)
    low_lane = lax.broadcasted_iota(jnp.int32, (rows, 2 * STATE), 1) < STATE
    bb = jnp.where(low_lane, state, turned)
    cc = jnp.where(low_lane, turned, state)
    bb_t = bb.T
    low_row = lax.broadcasted_iota(jnp.int32, (2 * STATE, rows), 0) < STATE

    loads["bias"].wait()
    loads["speed"].wait()
    loads["step", 0].wait()
    loads["step", 1].wait()
    raw = mm_nt(wstep_v[0], hid[0]) + mm_nt(wstep_v[1], hid[1])
    step_rows = 8
    raw = jnp.concatenate([raw, jnp.zeros((step_rows - heads, rows), F32)], axis=0)
    head_row = lax.broadcasted_iota(jnp.int32, (step_rows, rows), 0)
    bias_full = jnp.zeros((step_rows, rows), F32)
    speed_full = jnp.zeros((step_rows, rows), F32)
    for h in range(heads):
        bias_full = jnp.where(head_row == h, bias[h], bias_full)
        speed_full = jnp.where(head_row == h, speed[h], speed_full)
    shifted = raw + bias_full
    steps = jnp.maximum(shifted, 0.0) + jnp.log1p(jnp.exp(-jnp.abs(shifted)))
    place_row = me * rows + lax.broadcasted_iota(jnp.int32, (step_rows, rows), 1)
    ok_row = place_row < limit
    spike = jnp.where(jnp.broadcast_to(ids_row, (step_rows, rows)) == UNCLEAR, SPIKE, 0.0)
    decay = jnp.where(ok_row, spike - speed_full * steps, 0.0)
    used = jnp.where(ok_row, steps, 0.0)
    t_at = lax.broadcasted_iota(jnp.int32, (rows, rows), 0)
    s_at = lax.broadcasted_iota(jnp.int32, (rows, rows), 1)
    forward = exact_mm(decay, (t_at <= s_at).astype(F32).astype(BF16))
    backward = exact_mm(decay, (t_at >= s_at).astype(F32).astype(BF16))
    total = forward[:, rows - 1 : rows]
    first = backward[:, 0:1]
    weight_f = jnp.exp(jnp.minimum(total - forward, 0.0)) * used
    weight_r = jnp.exp(jnp.minimum(first - backward, 0.0)) * used
    passing = jnp.exp(total)
    columns = jnp.concatenate(
        [forward, backward, jnp.zeros((128 - 2 * step_rows, rows), F32)], axis=0
    ).T

    loads["scan", 1].wait()
    x_v[...] = silu(part_x[...] + mm(hid[1], wscan_v[1])).astype(BF16)

    for h in range(heads):
        lanes = slice(h * HEAD_DIM, (h + 1) * HEAD_DIM)
        scaled = bb_t * jnp.where(low_row, weight_f[h : h + 1], weight_r[h : h + 1])
        ends = mm(scaled.astype(BF16), x_v[:, lanes])
        endsend[h, 0:HEAD_DIM] = ends.astype(BF16)
        endsend[h, HEAD_DIM : HEAD_DIM + 16] = halves(
            jnp.broadcast_to(passing[h : h + 1], (8, HEAD_DIM))
        )

    def end_copy(k):
        to = lax.rem(member + k, heads)
        return pltpu.make_async_remote_copy(
            src_ref=endsend.at[to],
            dst_ref=endrecv.at[member],
            send_sem=en_ss.at[k],
            recv_sem=en_rs.at[k],
            device_id={"seq": base + to},
            device_id_type=MESH,
        )

    for k in range(1, heads):
        end_copy(k).start()
    endrecv[member] = endsend[member]

    loads["again"].wait()
    loads["sgain"].wait()
    pairing = mm_nt(jnp.where(low_lane, cc, 0.0).astype(BF16), bb.astype(BF16))
    pairing = jnp.where(t_at == s_at, 2.0 * pairing, pairing)
    for h in range(heads):
        lanes = slice(h * HEAD_DIM, (h + 1) * HEAD_DIM)
        gap = jnp.where(
            t_at >= s_at,
            columns[:, h : h + 1] - forward[h : h + 1],
            columns[:, step_rows + h : step_rows + h + 1] - backward[h : h + 1],
        )
        mixing = pairing * jnp.exp(jnp.minimum(gap, 0.0)) * used[h : h + 1]
        loc_v[:, lanes] = mm(mixing.astype(BF16), x_v[:, lanes])

    for k in range(1, heads):
        q_copy(k).wait()
    acc[...] = jnp.zeros_like(acc)
    scale = 2.0 / math.sqrt(HEAD_DIM) * math.log2(math.e)
    lane_rows = lax.broadcasted_iota(jnp.int32, (rows, HEAD_DIM), 0)

    def absorb(source):
        ones = (source * rows + lane_rows < limit).astype(F32).astype(BF16)
        key = kvrecv[source, 0]
        value = jnp.concatenate([kvrecv[source, 1], ones], axis=1)
        for m in range(heads):
            weights = jnp.exp2(mm_nt(qrecv[m], key) * scale).astype(BF16)
            acc[m] += mm(weights, value)

    absorb(me)

    def attend(t, carry):
        kv_copy(0, t).wait()
        kv_copy(1, t).wait()
        absorb(routed(t, -1))
        return carry

    def message(ref, i):
        whole = ref[i].astype(F32)
        factor = whole[HEAD_DIM : HEAD_DIM + 1] + whole[HEAD_DIM + 8 : HEAD_DIM + 9]
        return whole[:STATE], whole[STATE:HEAD_DIM], factor

    def run_copy(k):
        return pltpu.make_async_remote_copy(
            src_ref=runsend,
            dst_ref=runrecv.at[group],
            send_sem=ru_ss.at[k],
            recv_sem=ru_rs.at[k],
            device_id={"seq": lax.rem(group + k, group_count) * heads + member},
            device_id_type=MESH,
        )

    def ent_copy(k):
        to = lax.rem(member + k, heads)
        return pltpu.make_async_remote_copy(
            src_ref=entsend.at[to],
            dst_ref=entrecv.at[member],
            send_sem=er_ss.at[k],
            recv_sem=er_rs.at[k],
            device_id={"seq": base + to},
            device_id_type=MESH,
        )

    nothing = jnp.zeros((STATE, HEAD_DIM), F32)
    near_end = 3 * n // 8
    far_end = 5 * n // 8
    lax.fori_loop(0, near_end, attend, 0)

    for k in range(1, heads):
        end_copy(k).wait()
    run_f, run_r = nothing, nothing
    run_pass = jnp.ones((1, HEAD_DIM), F32)
    for b in range(heads):
        end_f, _, factor = message(endrecv, b)
        run_f = factor * run_f + end_f
        run_pass = run_pass * factor
        _, end_r, factor = message(endrecv, heads - 1 - b)
        run_r = factor * run_r + end_r
    runsend[0:STATE] = run_f.astype(BF16)
    runsend[STATE:HEAD_DIM] = run_r.astype(BF16)
    runsend[HEAD_DIM : HEAD_DIM + 16] = halves(jnp.broadcast_to(run_pass, (8, HEAD_DIM)))

    def run_start(k, carry):
        run_copy(k).start()
        return carry

    def run_wait(k, carry):
        run_copy(k).wait()
        return carry

    lax.fori_loop(1, group_count, run_start, 0)
    runrecv[group] = runsend[...]
    lax.fori_loop(near_end, far_end, attend, 0)

    lax.fori_loop(1, group_count, run_wait, 0)

    def lap(t, carry):
        enter_f, enter_r, product = carry
        end_f, _, factor = message(runrecv, lax.rem(group + t, group_count))
        _, end_r, factor_r = message(runrecv, lax.rem(group - t + group_count, group_count))
        return factor * enter_f + end_f, factor_r * enter_r + end_r, product * factor

    enter_f, enter_r, product = lax.fori_loop(
        0, group_count, lap, (nothing, nothing, jnp.ones((1, HEAD_DIM), F32))
    )
    enter_f = enter_f / (1.0 - product)
    enter_r = enter_r / (1.0 - product)
    for b in range(heads):
        entsend[b, 0:STATE] = enter_f.astype(BF16)
        end_f, _, factor = message(endrecv, b)
        enter_f = factor * enter_f + end_f
        back = heads - 1 - b
        entsend[back, STATE:HEAD_DIM] = enter_r.astype(BF16)
        _, end_r, factor = message(endrecv, back)
        enter_r = factor * enter_r + end_r
    for k in range(1, heads):
        ent_copy(k).start()
    entrecv[member] = entsend[member]
    lax.fori_loop(far_end, n - 1, attend, 0)
    for m in range(heads):
        attsend[m] = normed(acc[m, :, :HEAD_DIM] / acc[m, :, HEAD_DIM:]).astype(BF16)

    def att_copy(k):
        to = lax.rem(member + k, heads)
        return pltpu.make_async_remote_copy(
            src_ref=attsend.at[to],
            dst_ref=attrecv.at[member],
            send_sem=at_ss.at[k],
            recv_sem=at_rs.at[k],
            device_id={"seq": base + to},
            device_id_type=MESH,
        )

    for k in range(1, heads):
        att_copy(k).start()
    attrecv[member] = attsend[member]

    for k in range(1, heads):
        ent_copy(k).wait()
    for h in range(heads):
        lanes = slice(h * HEAD_DIM, (h + 1) * HEAD_DIM)
        reading = cc * jnp.exp(
            jnp.where(
                low_lane,
                columns[:, h : h + 1],
                columns[:, step_rows + h : step_rows + h + 1],
            )
        )
        entering = entrecv[h]
        loc_v[:, lanes] = normed(loc_v[:, lanes] + mm(reading.astype(BF16), entering)) * sgain[
            :, lanes
        ]

    for k in range(1, heads):
        att_copy(k).wait()
    for h in range(heads):
        lanes = slice(h * HEAD_DIM, (h + 1) * HEAD_DIM)
        comb_v[:, lanes] = (
            again[:, lanes] * attrecv[h].astype(F32) + loc_v[:, lanes]
        ).astype(BF16)

    loads["out", 0].wait()
    loads["out", 1].wait()
    combined = comb_v[...]
    pieces = psend.shape[0]
    width = half // pieces
    shares = []
    for p in range(pieces):
        psend[p] = mm(combined, wout_v[1, :, p * width : (p + 1) * width]).astype(BF16)
        share = pltpu.make_async_remote_copy(
            src_ref=psend.at[p],
            dst_ref=precv.at[p],
            send_sem=ps_ss.at[p],
            recv_sem=ps_rs.at[p],
            device_id={"chan": partner},
            device_id_type=MESH,
        )
        share.start()
        shares.append(share)
    for p in range(pieces):
        lanes = slice(p * width, (p + 1) * width)
        mine = stream[:, lanes].astype(F32) + mm(combined, wout_v[0, :, lanes])
        shares[p].wait()
        out[:, lanes] = (mine + precv[p].astype(F32)).astype(BF16)


def local(
    n,
    stream,
    ids,
    genome_length,
    embedding,
    attention_in,
    scan_input,
    state_maps,
    step_weight,
    step_bias,
    head_decay_speed,
    attention_gain,
    scan_gain,
    out_weight,
):
    rows, half = stream.shape
    heads = step_weight.shape[1]
    span = heads * HEAD_DIM
    groups = n // heads
    pieces = 4
    vmem = pl.BlockSpec(memory_space=pltpu.VMEM)
    anywhere = pl.BlockSpec(memory_space=pltpu.HBM)
    dma = pltpu.SemaphoreType.DMA
    V = pltpu.VMEM
    return pl.pallas_call(
        functools.partial(kernel, n),
        out_shape=jax.ShapeDtypeStruct((rows, half), BF16),
        in_specs=[anywhere] * 13,
        out_specs=vmem,
        scratch_shapes=[
            V((rows, half), BF16),
            V((1, rows), jnp.int32),
            pltpu.SMEM((1,), jnp.int32),
            pltpu.SMEM((heads,), F32),
            pltpu.SMEM((heads,), F32),
            V((1, span), F32),
            V((1, span), F32),
            V((2, 128, half), BF16),
            V((3, 2, half, span), BF16),
            V((2, half, span), BF16),
            V((2, half, 2 * STATE), BF16),
            V((2, heads, half), BF16),
            V((2, span, half), BF16),
            V((rows, half), BF16),
            V((2, rows, half), BF16),
            V((heads, 2, rows, HEAD_DIM), BF16),
            V((n, 2, rows, HEAD_DIM), BF16),
            V((heads, rows, HEAD_DIM), BF16),
            V((heads, rows, HEAD_DIM), BF16),
            V((heads, rows, 2 * HEAD_DIM), F32),
            V((heads, rows, HEAD_DIM), BF16),
            V((heads, rows, HEAD_DIM), BF16),
            V((heads, HEAD_DIM + 16, HEAD_DIM), BF16),
            V((heads, HEAD_DIM + 16, HEAD_DIM), BF16),
            V((HEAD_DIM + 16, HEAD_DIM), BF16),
            V((groups, HEAD_DIM + 16, HEAD_DIM), BF16),
            V((heads, HEAD_DIM, HEAD_DIM), BF16),
            V((heads, HEAD_DIM, HEAD_DIM), BF16),
            V((rows, span), F32),
            V((rows, span), F32),
            V((rows, span), F32),
            V((rows, span), F32),
            V((rows, half), F32),
            V((rows, span), BF16),
            V((rows, span), F32),
            V((rows, span), BF16),
            V((pieces, rows, half // pieces), BF16),
            V((pieces, rows, half // pieces), BF16),
            dma((23,)),
            dma,
            dma,
            dma((2, n)),
            dma((2, n)),
            dma((heads,)),
            dma((heads,)),
            dma((heads,)),
            dma((heads,)),
            dma((heads,)),
            dma((heads,)),
            dma((groups,)),
            dma((groups,)),
            dma((heads,)),
            dma((heads,)),
            dma((pieces,)),
            dma((pieces,)),
        ],
        compiler_params=pltpu.CompilerParams(
            collective_id=0, has_side_effects=True, vmem_limit_bytes=60 * 1024 * 1024
        ),
    )(
        stream,
        ids.reshape(1, rows),
        genome_length,
        embedding,
        jnp.transpose(attention_in, (1, 0, 2)),
        scan_input,
        state_maps,
        step_weight.T,
        step_bias,
        head_decay_speed,
        attention_gain.reshape(1, span),
        scan_gain.reshape(1, span),
        out_weight,
    )


def solution(mesh):
    placed = (
        P(("groups", "seq"), "chan"),
        P(("groups", "seq")),
        P("groups"),
        P(),
        P(None, None, "chan"),
        P(None, "chan"),
        P(None, "chan"),
        P(None, "chan"),
        P("chan"),
        P("chan"),
        P("chan"),
        P("chan"),
        P("chan", None),
    )
    return jax.shard_map(
        functools.partial(local, mesh.shape["seq"]),
        mesh=mesh,
        in_specs=placed,
        out_specs=P(("groups", "seq"), "chan"),
        check_vma=False,
    )
```
